32 devices in a mesh: space: 16 (over z, x, core), ens: 2 (over y).
Axes of the slice: x: 2, y: 2, z: 4, core: 2. Of those that a mesh axis runs over, the one named last changes fastest.
Arguments:
- params: float32 [64, 256, 512], P('ens', 'space'), may hold values from 0.55 to 0.8
- base_thickness: float32 [256, 512], P('space'), may hold values from 0.5 to 3
- balance: float32 [256, 512], P('space'), may hold values from -0.1 to 0.3
- step_count: int32 [64], replicated, may hold values from 8 to 32, as said below
- obs_index: int32 [4096], P('space'), may hold values from 0 to 8191
- observed: float32 [4096], P('space'), may hold values from 0.5 to 2
- noise_var: float32 [4096], P('space'), may hold values from 0.5 to 4
Outputs:
- thickness: float32 [64, 256, 512], P('ens', 'space')
- updated: float32 [64, 256, 512], P('ens', 'space')
The draws below stay inside these ranges and needn't reach their ends.
Inputs may be any that keep to these rules, and one draw needn't show every extreme that they name: `step_count`: some member runs exactly 32 steps.
All inputs are finite; a program needn't handle non-finite values.
Results may differ from the reference program's by a relative error of at most 0.000074.
Values sent between devices are 32-bit elements; how exact they have to be, the bound alone decides.
A program may use at most 64 MiB of HBM per device.

```python
import math
import jax
import jax.numpy as jnp
from jax import lax

MEMBERS = 64
CX = 16
NY = 512
OBS_DEV = 256
STEPS = 32
NX = 256
NOBS = 4096


def draw_step_count(key, part):
    first_key, second_key = jax.random.split(jax.random.fold_in(key, 17))
    counts = jax.random.randint(first_key, (MEMBERS,), STEPS // 4, STEPS + 1)
    chosen = jax.random.randint(second_key, (), 0, MEMBERS)
    counts = counts.at[chosen].set(STEPS)
    return counts.astype(jnp.int32)


def draw_params(key, part):
    first_key = jax.random.fold_in(jax.random.fold_in(key, 29), 0)
    shape = (MEMBERS, NX, NY)
    values = jax.random.uniform(first_key, shape, jnp.float32, 0.55, 0.8)
    return values.astype(jnp.float32)


def draw_base_thickness(key, part):
    phase_key, level_key, jitter_key = jax.random.split(jax.random.fold_in(key, 31), 3)
    phase = jax.random.uniform(phase_key, (), jnp.float32, 0.0, 2.0 * math.pi)
    row_pos = jnp.arange(NX, dtype=jnp.float32)[:, None]
    period = 12.0
    high_share = 0.5
    wave = 0.3 * jnp.sin(2.0 * math.pi * row_pos / period + phase)
    upper = jax.random.bernoulli(level_key, high_share, (NX, NY))
    jitter = jax.random.uniform(jitter_key, (NX, NY), jnp.float32, 0.0, 1.0)
    low_value = 0.8 + 0.4 * jitter
    high_value = 2.2 + 0.5 * jitter
    values = jnp.where(upper, high_value, low_value) + wave
    return jnp.clip(values, 0.5, 3.0).astype(jnp.float32)


def touch_ends(array, rng, smallest, largest):
    shape = array.shape
    spot = [jax.random.randint(jax.random.fold_in(rng, axis), (), 0, shape[axis]) for axis in range(len(shape))]
    array = array.at[tuple(spot)].set(smallest)
    longest = shape.index(max(shape))
    spot[longest] = (spot[longest] + 1) % shape[longest]
    return array.at[tuple(spot)].set(largest)


def block_levels(own_key, shape, cuts, low, top_value):
    def one(position, parts):
        draws = jax.random.uniform(jax.random.fold_in(jax.random.fold_in(own_key, 6), position), (parts,), jnp.float32, low / len(cuts), top_value / len(cuts))
        return jnp.repeat(jnp.exp(draws), shape[position] // parts).reshape((-1,) + (1,) * (len(shape) - position - 1))

    factor_of = one(*cuts[0])
    for cut in cuts[1:]:
        factor_of = factor_of * one(*cut)
    return factor_of


def setup_inputs(seed: int = 0) -> dict:
    arg_keys = jax.random.split(jax.random.key(seed), 8)
    params = draw_params(jax.random.fold_in(arg_keys[7], 71), 0)
    base_thickness = draw_base_thickness(jax.random.fold_in(arg_keys[7], 71), 0)
    balance = jnp.clip(-0.1 + 0.4 * jax.random.uniform(arg_keys[2], (NX, NY), jnp.float32) ** block_levels(arg_keys[2], (NX, NY), ((0, 16),), -0.2, 0.2), -0.1, 0.3)
    step_count = draw_step_count(jax.random.fold_in(arg_keys[7], 71), 0)
    obs_index = touch_ends(jax.random.randint(arg_keys[4], (NOBS,), 0, CX * NY), jax.random.fold_in(arg_keys[4], 1), 0, (CX * NY) - 1).astype(jnp.int32)
    observed = jnp.clip(0.5 + 1.5 * jax.random.uniform(arg_keys[5], (NOBS,), jnp.float32) ** block_levels(arg_keys[5], (NOBS,), ((0, 16),), -0.2, 0.2), 0.5, 2.0)
    noise_var = jnp.clip(jnp.exp(math.log(4.0) - 2.0794415 * jax.random.uniform(arg_keys[6], (NOBS,), jnp.float32) ** block_levels(arg_keys[6], (NOBS,), ((0, 16),), -0.2, 0.2)), 0.5, 4.0)
    return {"params": params, "base_thickness": base_thickness, "balance": balance, "step_count": step_count, "obs_index": obs_index, "observed": observed, "noise_var": noise_var}


time_step = 0.11

def stencil(padded, slip_padded, thickness, balance):
    diffusivity = slip_padded * padded * padded / (1.0 + padded * padded)
    centre = diffusivity[:, 1:-1, 1:-1]
    divergence = jnp.zeros_like(thickness)
    for row_part, col_part in ((slice(2, None), slice(1, -1)), (slice(None, -2), slice(1, -1)), (slice(1, -1), slice(2, None)), (slice(1, -1), slice(None, -2))):
        divergence = divergence + 0.5 * (diffusivity[:, row_part, col_part] + centre) * (padded[:, row_part, col_part] - thickness)
    return thickness + time_step * (divergence + balance)

def ensemble_terms(predicted, observed, noise_var):
    members = predicted.shape[0]
    scaling = lax.rsqrt(noise_var)
    average = lax.optimization_barrier(jnp.mean(predicted, axis=0))
    anomalies = (predicted - average) * scaling / jnp.sqrt(jnp.float32(members - 1))
    mismatch = (observed - predicted) * scaling
    gram = jnp.dot(anomalies, anomalies.T, precision=lax.Precision.HIGHEST)
    cross = jnp.dot(anomalies, mismatch.T, precision=lax.Precision.HIGHEST)
    return (gram, cross)

def solve_weights(gram, cross):
    members = gram.shape[0]
    factor = jnp.linalg.cholesky(gram + jnp.eye(members, dtype=gram.dtype))
    inner = lax.linalg.triangular_solve(factor, cross, left_side=True, lower=True)
    result = lax.linalg.triangular_solve(factor, inner, left_side=True, lower=True, transpose_a=True)
    return result / jnp.sqrt(jnp.float32(members - 1))

def reference(params, base_thickness, balance, step_count, obs_index, observed, noise_var):
    members = params.shape[0]
    slip_padded = jnp.pad(jnp.exp(params), ((0, 0), (1, 1), (1, 1)))

    def advance(step_index, thickness):
        padded = jnp.pad(thickness, ((0, 0), (1, 1), (1, 1)))
        moved = stencil(padded, slip_padded, thickness, balance)
        return jnp.where((step_index < step_count)[:, None, None], moved, thickness)
    initial = jnp.broadcast_to(base_thickness[None], params.shape).astype(jnp.float32)
    thickness = lax.fori_loop(0, STEPS, advance, initial)
    block_of = (jnp.arange(NOBS) // OBS_DEV).astype(jnp.int32)
    cell_index = (block_of * (CX * NY) + obs_index).astype(jnp.int32)
    predicted = thickness.reshape(members, NX * NY)[:, cell_index]
    gram, cross = ensemble_terms(predicted, observed, noise_var)
    weights = solve_weights(gram, cross)
    deviation = params - lax.optimization_barrier(jnp.mean(params, axis=0))
    increment = jnp.dot(weights.T, deviation.reshape(members, NX * NY), precision=lax.Precision.HIGHEST)
    updated = params + increment.reshape(params.shape)
    return (thickness, updated)
```

```python
import functools
import jax
import jax.numpy as jnp
from jax import lax
from jax.experimental import pallas as pl
from jax.experimental.pallas import tpu as pltpu
from jax.sharding import PartitionSpec as P

time_step = 0.11
steps = 32
halo = 4
sub = 8
lane = 128
MESH = pl.DeviceIdType.MESH


def reciprocal(x):
    r = pl.reciprocal(x, approx=True)
    return r * (2.0 - x * r)


def substep(h_ref, slip_ref, bal_ref, group, first, last, masks, rows):
    pieces = h_ref.shape[-1] // lane
    lanes = lax.broadcasted_iota(jnp.int32, (sub, lane), 1)
    at_end = lanes == lane - 1
    at_start = lanes == 0
    cols = [pl.ds(p * lane, lane) for p in range(pieces)]
    zero = jnp.zeros((sub, lane), jnp.float32)
    prev = None
    for row in range(first, last):
        h = [h_ref[group, row, :, c] for c in cols]
        d = []
        for p, c in enumerate(cols):
            square = h[p] * h[p]
            d.append(slip_ref[group, row, :, c] * square * reciprocal(1.0 + square))
        if prev is not None:
            prev_h, prev_d, prev_down = prev
            down = [(d[p] + prev_d[p]) * (h[p] - prev_h[p]) for p in range(pieces)]
            if prev_down is not None:
                out = row - 1
                mask = masks[0] if out < halo else masks[1] if out < halo + rows else masks[2]
                h_rot = [pltpu.roll(prev_h[p], lane - 1, 1) for p in range(pieces)] + [zero]
                d_rot = [pltpu.roll(prev_d[p], lane - 1, 1) for p in range(pieces)] + [zero]
                flux = []
                for p in range(pieces):
                    h_right = jnp.where(at_end, h_rot[p + 1], h_rot[p])
                    d_right = jnp.where(at_end, d_rot[p + 1], d_rot[p])
                    flux.append((d_right + prev_d[p]) * (h_right - prev_h[p]))
                f_rot = [pltpu.roll(flux[p], 1, 1) for p in range(pieces)]
                for p, c in enumerate(cols):
                    edge = prev_d[0] * prev_h[0] if p == 0 else f_rot[p - 1]
                    f_left = jnp.where(at_start, edge, f_rot[p])
                    change = (down[p] - prev_down[p]) + (flux[p] - f_left)
                    moved = (prev_h[p] + bal_ref[out, :, c]) + change
                    h_ref[group, out, :, c] = jnp.where(mask, moved, prev_h[p])
        else:
            down = None
        prev = (h, d, down)


def advance_kernel(
    spaces, enss, params_ref, params_any, bb_ref, count_ref, out_ref, gathered,
    h_ref, slip_ref, bal_ref, land_ref, bb_land,
    send_sem, recv_sem, slip_send, slip_recv, bb_send, bb_recv, ens_send, ens_recv, own_sem,
):
    members, rows, width = params_ref.shape
    groups = members // sub
    total = rows + 2 * halo
    blocks = steps // halo
    me = lax.axis_index("space")
    ens = lax.axis_index("ens")
    has_up = me > 0
    has_down = me < spaces - 1
    up = jnp.maximum(me - 1, 0)
    down = jnp.minimum(me + 1, spaces - 1)
    others = [lax.rem(ens + step, enss) for step in range(1, enss)]

    barrier = pltpu.get_barrier_semaphore()

    @pl.when(has_up)
    def _():
        pl.semaphore_signal(barrier, inc=1, device_id={"space": up}, device_id_type=MESH)

    @pl.when(has_down)
    def _():
        pl.semaphore_signal(barrier, inc=1, device_id={"space": down}, device_id_type=MESH)

    for other in others:
        pl.semaphore_signal(barrier, inc=1, device_id={"ens": other}, device_id_type=MESH)
    neighbours = has_up.astype(jnp.int32) + has_down.astype(jnp.int32) + (enss - 1)
    pl.semaphore_wait(barrier, neighbours)

    sides = (
        (has_up, up, pl.ds(halo, halo), pl.ds(halo + rows, halo), 1),
        (has_down, down, pl.ds(rows, halo), pl.ds(0, halo), 0),
    )
    own_rows = (pl.ds(0, halo), pl.ds(rows - halo, halo))

    def bb_copy(side):
        _, target, _, _, there = sides[side]
        return pltpu.make_async_remote_copy(
            bb_ref.at[own_rows[side]], bb_land.at[there], bb_send.at[side], bb_recv.at[there],
            device_id={"space": target}, device_id_type=MESH,
        )

    def slip_copy(group, side):
        _, target, source, dest, there = sides[side]
        return pltpu.make_async_remote_copy(
            slip_ref.at[group, source], slip_ref.at[group, dest],
            slip_send.at[group, side], slip_recv.at[group, there],
            device_id={"space": target}, device_id_type=MESH,
        )

    def slip_arrival(group, side):
        _, target, _, _, _ = sides[side]
        here = pl.ds(0, halo) if side == 0 else pl.ds(halo + rows, halo)
        return pltpu.make_async_remote_copy(
            slip_ref.at[group, here], slip_ref.at[group, here],
            slip_send.at[group, side], slip_recv.at[group, side],
            device_id={"space": target}, device_id_type=MESH,
        )

    def h_copy(group, side, slot):
        _, target, source, _, there = sides[side]
        return pltpu.make_async_remote_copy(
            h_ref.at[group, source], land_ref.at[group, slot, there],
            send_sem.at[group, side], recv_sem.at[group, slot, there],
            device_id={"space": target}, device_id_type=MESH,
        )

    def h_arrival(group, side, slot):
        _, target, source, _, _ = sides[side]
        return pltpu.make_async_remote_copy(
            h_ref.at[group, source], land_ref.at[group, slot, side],
            send_sem.at[group, side], recv_sem.at[group, slot, side],
            device_id={"space": target}, device_id_type=MESH,
        )

    def bb_arrival(side):
        _, target, _, _, _ = sides[side]
        return pltpu.make_async_remote_copy(
            bb_ref.at[own_rows[side]], bb_land.at[side], bb_send.at[side], bb_recv.at[side],
            device_id={"space": target}, device_id_type=MESH,
        )

    for side in range(2):
        @pl.when(sides[side][0])
        def _(side=side):
            bb_copy(side).start()

    @pl.loop(0, groups)
    def _(group):
        block = params_ref[pl.ds(group * sub, sub)]
        turned = jnp.swapaxes(jnp.exp(block) * (0.5 * time_step), 0, 1)
        slip_ref[group, pl.ds(halo, rows)] = turned
        for side in range(2):
            @pl.when(sides[side][0])
            def _(side=side):
                slip_copy(group, side).start()

    def ens_copy(step):
        return pltpu.make_async_remote_copy(
            params_any, gathered.at[ens], ens_send.at[step], ens_recv.at[step],
            device_id={"ens": others[step]}, device_id_type=MESH,
        )

    for step in range(enss - 1):
        ens_copy(step).start()
    own_copy = pltpu.make_async_copy(params_ref, gathered.at[ens], own_sem)
    own_copy.start()

    def wide(row):
        return jnp.broadcast_to(row, (sub, width))

    @pl.loop(0, rows)
    def _(row):
        base = wide(bb_ref[row, 0:1, :])
        for group in range(groups):
            h_ref[group, row + halo] = base
        bal_ref[row + halo] = wide(bb_ref[row, 1:2, :]) * time_step

    for side in range(2):
        begin = 0 if side == 0 else halo + rows

        @pl.when(sides[side][0])
        def _(side=side, begin=begin):
            bb_arrival(side).wait_recv()
            for row in range(halo):
                base = wide(bb_land[side, row, 0:1, :])
                for group in range(groups):
                    h_ref[group, begin + row] = base
                bal_ref[begin + row] = wide(bb_land[side, row, 1:2, :]) * time_step

        @pl.when(jnp.logical_not(sides[side][0]))
        def _(side=side, begin=begin):
            zero = jnp.zeros((sub, width), jnp.float32)
            for row in range(halo):
                for group in range(groups):
                    h_ref[group, begin + row] = zero
                    slip_ref[group, begin + row] = zero
                bal_ref[begin + row] = zero

    @pl.loop(0, blocks)
    def _(block):
        slot = lax.rem(block, 2)

        @pl.loop(0, groups)
        def _(group):
            for side in range(2):
                begin = 0 if side == 0 else halo + rows

                @pl.when(jnp.logical_and(sides[side][0], block == 0))
                def _(side=side):
                    slip_arrival(group, side).wait_recv()

                @pl.when(jnp.logical_and(sides[side][0], block > 0))
                def _(side=side, begin=begin):
                    h_copy(group, side, slot).wait_send()
                    h_arrival(group, side, slot).wait_recv()
                    h_ref[group, pl.ds(begin, halo)] = land_ref[group, slot, side]

            count = count_ref[group]
            counts = (
                count * has_up.astype(jnp.int32), count, count * has_down.astype(jnp.int32)
            )
            for step in range(halo):
                now = block * halo + step
                masks = [now < value for value in counts]
                substep(h_ref, slip_ref, bal_ref, group, step, total - step, masks, rows)

            for side in range(2):
                @pl.when(jnp.logical_and(sides[side][0], block < blocks - 1))
                def _(side=side):
                    h_copy(group, side, 1 - slot).start()

    for group in range(groups):
        out_ref[pl.ds(group * sub, sub)] = jnp.swapaxes(h_ref[group, pl.ds(halo, rows)], 0, 1)

    own_copy.wait()
    for step in range(enss - 1):
        ens_copy(step).wait()
    for side in range(2):
        @pl.when(sides[side][0])
        def _(side=side):
            bb_copy(side).wait_send()
            for group in range(groups):
                slip_copy(group, side).wait_send()


def advance(params, bb, counts, spaces, enss):
    members, rows, width = params.shape
    groups = members // sub
    total = rows + 2 * halo
    dma = pltpu.SemaphoreType.DMA
    vmem = pl.BlockSpec(memory_space=pltpu.VMEM)
    hbm = pl.BlockSpec(memory_space=pl.ANY)
    return pl.pallas_call(
        functools.partial(advance_kernel, spaces, enss),
        out_shape=(
            jax.ShapeDtypeStruct(params.shape, jnp.float32),
            jax.ShapeDtypeStruct((enss, members, rows, width), jnp.float32),
        ),
        in_specs=[vmem, hbm, vmem, vmem],
        out_specs=(vmem, hbm),
        scratch_shapes=[
            pltpu.VMEM((groups, total, sub, width), jnp.float32),
            pltpu.VMEM((groups, total, sub, width), jnp.float32),
            pltpu.VMEM((total, sub, width), jnp.float32),
            pltpu.VMEM((groups, 2, 2, halo, sub, width), jnp.float32),
            pltpu.VMEM((2, halo, 2, width), jnp.float32),
            dma((groups, 2)),
            dma((groups, 2, 2)),
            dma((groups, 2)),
            dma((groups, 2)),
            dma((2,)),
            dma((2,)),
            dma((max(enss - 1, 1),)),
            dma((max(enss - 1, 1),)),
            dma(()),
        ],
        compiler_params=pltpu.CompilerParams(
            collective_id=0, has_side_effects=True, vmem_limit_bytes=40 * 1024 * 1024
        ),
        name="advance",
    )(params, params, bb, counts)


def ensemble_terms(predicted, observed, noise_var):
    members = predicted.shape[0]
    scaling = lax.rsqrt(noise_var)
    average = jnp.mean(predicted, axis=0)
    anomalies = (predicted - average) * scaling / jnp.sqrt(jnp.float32(members - 1))
    mismatch = (observed - predicted) * scaling
    gram = jnp.dot(anomalies, anomalies.T, precision=lax.Precision.HIGHEST)
    cross = jnp.dot(anomalies, mismatch.T, precision=lax.Precision.HIGHEST)
    return (gram, cross)


def solve_weights(gram, cross):
    members = gram.shape[0]
    factor = jnp.linalg.cholesky(gram + jnp.eye(members, dtype=gram.dtype))
    inner = lax.linalg.triangular_solve(factor, cross, left_side=True, lower=True)
    result = lax.linalg.triangular_solve(
        factor, inner, left_side=True, lower=True, transpose_a=True
    )
    return result / jnp.sqrt(jnp.float32(members - 1))


def shards(params, base_thickness, balance, step_count, obs_index, observed, noise_var):
    members_dev = params.shape[0]
    ens_index = lax.axis_index("ens")
    enss = lax.axis_size("ens")
    members = members_dev * enss
    own_counts = lax.dynamic_slice_in_dim(step_count, ens_index * members_dev, members_dev)
    counts = jnp.broadcast_to(
        own_counts.reshape(members_dev // sub, sub, 1), (members_dev // sub, sub, lane)
    )
    bb = jnp.stack([base_thickness, balance], axis=1)
    thickness, gathered = advance(params, bb, counts, lax.axis_size("space"), enss)
    tile_cells = params.shape[1] * params.shape[2]
    predicted = jnp.take(thickness.reshape(members_dev, tile_cells), obs_index, axis=1)
    obs_block = lax.all_to_all(predicted, "ens", split_axis=1, concat_axis=0, tiled=True)
    block_width = obs_block.shape[1]
    observed_part = lax.dynamic_slice_in_dim(observed, ens_index * block_width, block_width)
    noise_part = lax.dynamic_slice_in_dim(noise_var, ens_index * block_width, block_width)
    gram, cross = ensemble_terms(obs_block, observed_part, noise_part)
    gram, cross = lax.psum((gram, cross), ("space", "ens"))
    weights = solve_weights(gram, cross)
    weight_cols = lax.dynamic_slice_in_dim(weights, ens_index * members_dev, members_dev, 1)
    flat_piece = gathered.reshape(members, tile_cells)
    weighted = jnp.dot(weight_cols.T, flat_piece, precision=lax.Precision.HIGHEST)
    member_total = jnp.sum(flat_piece, axis=0)
    column_sums = jnp.sum(weight_cols, axis=0)
    increment = weighted - column_sums[:, None] * member_total[None, :] / members
    updated = params + increment.reshape(params.shape)
    return (thickness, updated)


def solution(mesh):
    in_specs = (
        P("ens", "space", None),
        P("space", None),
        P("space", None),
        P(),
        P("space"),
        P("space"),
        P("space"),
    )
    out_specs = (P("ens", "space", None), P("ens", "space", None))
    return jax.shard_map(shards, mesh=mesh, in_specs=in_specs, out_specs=out_specs, check_vma=False)
```

```python
import functools
import jax
import jax.numpy as jnp
from jax import lax
from jax.experimental import pallas as pl
from jax.experimental.pallas import tpu as pltpu
from jax.sharding import PartitionSpec as P

time_step = 0.11
steps = 32
halo = 1
sub = 8
lane = 128
MESH = pl.DeviceIdType.MESH


def reciprocal(x):
    r = pl.reciprocal(x, approx=True)
    return r * (2.0 - x * r)


def dot(left, right, right_dim):
    return lax.dot_general(
        left, right, (((1,), (right_dim,)), ((), ())),
        precision=lax.Precision.HIGHEST, preferred_element_type=jnp.float32,
    )


def substep(h_ref, slip_ref, bal_ref, group, first, last, masks, rows):
    pieces = h_ref.shape[-1] // lane
    lanes = lax.broadcasted_iota(jnp.int32, (sub, lane), 1)
    at_end = lanes == lane - 1
    at_start = lanes == 0
    cols = [pl.ds(p * lane, lane) for p in range(pieces)]
    zero = jnp.zeros((sub, lane), jnp.float32)
    prev = None
    for row in range(first, last):
        h = [h_ref[group, row, :, c] for c in cols]
        d = []
        for p, c in enumerate(cols):
            square = h[p] * h[p]
            d.append(slip_ref[group, row, :, c] * square * reciprocal(1.0 + square))
        if prev is not None:
            prev_h, prev_d, prev_down = prev
            down = [(d[p] + prev_d[p]) * (h[p] - prev_h[p]) for p in range(pieces)]
            if prev_down is not None:
                out = row - 1
                mask = masks[0] if out < halo else masks[1] if out < halo + rows else masks[2]
                h_rot = [pltpu.roll(prev_h[p], lane - 1, 1) for p in range(pieces)] + [zero]
                d_rot = [pltpu.roll(prev_d[p], lane - 1, 1) for p in range(pieces)] + [zero]
                flux = []
                for p in range(pieces):
                    h_right = jnp.where(at_end, h_rot[p + 1], h_rot[p])
                    d_right = jnp.where(at_end, d_rot[p + 1], d_rot[p])
                    flux.append((d_right + prev_d[p]) * (h_right - prev_h[p]))
                f_rot = [pltpu.roll(flux[p], 1, 1) for p in range(pieces)]
                for p, c in enumerate(cols):
                    edge = prev_d[0] * prev_h[0] if p == 0 else f_rot[p - 1]
                    f_left = jnp.where(at_start, edge, f_rot[p])
                    change = (down[p] - prev_down[p]) + (flux[p] - f_left)
                    moved = (prev_h[p] + bal_ref[out, :, c]) + change
                    h_ref[group, out, :, c] = jnp.where(mask, moved, prev_h[p])
        else:
            down = None
        prev = (h, d, down)


def advance_kernel(
    spaces, enss, params_ref, bb_ref, count_ref, cell_ref, observed_ref, noise_ref, out_ref, updated_ref,
    h_ref, slip_ref, bal_ref, land_ref, bb_land, par_ref, pred_ref, sum_ref, sum_land,
    send_sem, recv_sem, slip_send, slip_recv, bb_send, bb_recv, ens_send, ens_recv,
    pred_send, pred_recv, sum_send, sum_recv,
):
    members, rows, width = params_ref.shape
    groups = members // sub
    total = rows + 2 * halo
    blocks = steps // halo
    me = lax.axis_index("space")
    ens = lax.axis_index("ens")
    has_up = me > 0
    has_down = me < spaces - 1
    up = jnp.maximum(me - 1, 0)
    down = jnp.minimum(me + 1, spaces - 1)
    others = [lax.rem(ens + step, enss) for step in range(1, enss)]
    stages = spaces.bit_length() - 1
    partners = []
    for stage in range(stages):
        bit = 1 << stage
        partners.append(me + bit - 2 * bit * lax.rem(lax.div(me, bit), 2))

    barrier = pltpu.get_barrier_semaphore()

    @pl.when(has_up)
    def _():
        pl.semaphore_signal(barrier, inc=1, device_id={"space": up}, device_id_type=MESH)

    @pl.when(has_down)
    def _():
        pl.semaphore_signal(barrier, inc=1, device_id={"space": down}, device_id_type=MESH)

    for other in others:
        pl.semaphore_signal(barrier, inc=1, device_id={"ens": other}, device_id_type=MESH)
    for partner in partners:
        pl.semaphore_signal(barrier, inc=1, device_id={"space": partner}, device_id_type=MESH)
    neighbours = has_up.astype(jnp.int32) + has_down.astype(jnp.int32) + (enss - 1) + stages
    pl.semaphore_wait(barrier, neighbours)

    sides = (
        (has_up, up, pl.ds(halo, halo), pl.ds(halo + rows, halo), 1),
        (has_down, down, pl.ds(rows, halo), pl.ds(0, halo), 0),
    )
    own_rows = (pl.ds(0, halo), pl.ds(rows - halo, halo))

    def bb_copy(side):
        _, target, _, _, there = sides[side]
        return pltpu.make_async_remote_copy(
            bb_ref.at[own_rows[side]], bb_land.at[there], bb_send.at[side], bb_recv.at[there],
            device_id={"space": target}, device_id_type=MESH,
        )

    def slip_copy(group, side):
        _, target, source, dest, there = sides[side]
        return pltpu.make_async_remote_copy(
            slip_ref.at[group, source], slip_ref.at[group, dest],
            slip_send.at[group, side], slip_recv.at[group, there],
            device_id={"space": target}, device_id_type=MESH,
        )

    def slip_arrival(group, side):
        _, target, _, _, _ = sides[side]
        here = pl.ds(0, halo) if side == 0 else pl.ds(halo + rows, halo)
        return pltpu.make_async_remote_copy(
            slip_ref.at[group, here], slip_ref.at[group, here],
            slip_send.at[group, side], slip_recv.at[group, side],
            device_id={"space": target}, device_id_type=MESH,
        )

    def h_copy(group, side, slot):
        _, target, source, _, there = sides[side]
        return pltpu.make_async_remote_copy(
            h_ref.at[group, source], land_ref.at[group, slot, there],
            send_sem.at[group, side], recv_sem.at[group, slot, there],
            device_id={"space": target}, device_id_type=MESH,
        )

    def h_arrival(group, side, slot):
        _, target, source, _, _ = sides[side]
        return pltpu.make_async_remote_copy(
            h_ref.at[group, source], land_ref.at[group, slot, side],
            send_sem.at[group, side], recv_sem.at[group, slot, side],
            device_id={"space": target}, device_id_type=MESH,
        )

    def bb_arrival(side):
        _, target, _, _, _ = sides[side]
        return pltpu.make_async_remote_copy(
            bb_ref.at[own_rows[side]], bb_land.at[side], bb_send.at[side], bb_recv.at[side],
            device_id={"space": target}, device_id_type=MESH,
        )

    for side in range(2):
        @pl.when(sides[side][0])
        def _(side=side):
            bb_copy(side).start()

    @pl.loop(0, groups)
    def _(group):
        turned = jnp.swapaxes(params_ref[pl.ds(group * sub, sub)], 0, 1)
        par_ref[ens * groups + group] = turned
        slip_ref[group, pl.ds(halo, rows)] = jnp.exp(turned) * (0.5 * time_step)
        for side in range(2):
            @pl.when(sides[side][0])
            def _(side=side):
                slip_copy(group, side).start()

    own_groups = pl.ds(ens * groups, groups)

    def ens_copy(step):
        return pltpu.make_async_remote_copy(
            par_ref.at[own_groups], par_ref.at[own_groups], ens_send.at[step], ens_recv.at[step],
            device_id={"ens": others[step]}, device_id_type=MESH,
        )

    for step in range(enss - 1):
        ens_copy(step).start()

    def wide(row):
        return jnp.broadcast_to(row, (sub, width))

    @pl.loop(0, rows)
    def _(row):
        base = wide(bb_ref[row, 0:1, :])
        for group in range(groups):
            h_ref[group, row + halo] = base
        bal_ref[row + halo] = wide(bb_ref[row, 1:2, :]) * time_step

    for side in range(2):
        begin = 0 if side == 0 else halo + rows

        @pl.when(sides[side][0])
        def _(side=side, begin=begin):
            bb_arrival(side).wait_recv()
            for row in range(halo):
                base = wide(bb_land[side, row, 0:1, :])
                for group in range(groups):
                    h_ref[group, begin + row] = base
                bal_ref[begin + row] = wide(bb_land[side, row, 1:2, :]) * time_step

        @pl.when(jnp.logical_not(sides[side][0]))
        def _(side=side, begin=begin):
            zero = jnp.zeros((sub, width), jnp.float32)
            for row in range(halo):
                for group in range(groups):
                    h_ref[group, begin + row] = zero
                    slip_ref[group, begin + row] = zero
                bal_ref[begin + row] = zero

    @pl.loop(0, blocks)
    def _(block):
        slot = lax.rem(block, 2)

        @pl.loop(0, groups)
        def _(group):
            for side in range(2):
                begin = 0 if side == 0 else halo + rows

                @pl.when(jnp.logical_and(sides[side][0], block == 0))
                def _(side=side):
                    slip_arrival(group, side).wait_recv()

                @pl.when(jnp.logical_and(sides[side][0], block > 0))
                def _(side=side, begin=begin):
                    h_copy(group, side, slot).wait_send()
                    h_arrival(group, side, slot).wait_recv()
                    h_ref[group, pl.ds(begin, halo)] = land_ref[group, slot, side]

            count = count_ref[group]
            counts = (
                count * has_up.astype(jnp.int32), count, count * has_down.astype(jnp.int32)
            )
            for step in range(halo):
                now = block * halo + step
                masks = [now < value for value in counts]
                substep(h_ref, slip_ref, bal_ref, group, step, total - step, masks, rows)

            for side in range(2):
                @pl.when(jnp.logical_and(sides[side][0], block < blocks - 1))
                def _(side=side):
                    h_copy(group, side, 1 - slot).start()

    for side in range(2):
        @pl.when(sides[side][0])
        def _(side=side):
            for group in range(groups):
                slip_copy(group, side).wait_send()

    cell_row = cell_ref[0:1, :]
    cell_col = cell_ref[1:2, :]
    count_obs = cell_ref.shape[1]
    one_hot = jnp.where(
        lax.broadcasted_iota(jnp.int32, (width, count_obs), 0) == cell_col, 1.0, 0.0
    )
    at_row = lax.broadcasted_iota(jnp.int32, (rows, sub, count_obs), 0) == cell_row
    for group in range(groups):
        cells = h_ref[group, pl.ds(halo, rows)].reshape(rows * sub, width)
        picked = dot(cells, one_hot, 0).reshape(rows, sub, count_obs)
        pred_ref[ens, pl.ds(group * sub, sub)] = jnp.sum(jnp.where(at_row, picked, 0.0), axis=0)

    def pred_copy(step):
        return pltpu.make_async_remote_copy(
            pred_ref.at[ens], pred_ref.at[ens], pred_send.at[step], pred_recv.at[step],
            device_id={"ens": others[step]}, device_id_type=MESH,
        )

    for step in range(enss - 1):
        pred_copy(step).start()
    for group in range(groups):
        out_ref[pl.ds(group * sub, sub)] = jnp.swapaxes(h_ref[group, pl.ds(halo, rows)], 0, 1)
    for step in range(enss - 1):
        pred_copy(step).wait()

    every = enss * members
    scaling = lax.rsqrt(noise_ref[...])
    predicted = pred_ref[...].reshape(every, count_obs)
    average = jnp.sum(predicted, axis=0, keepdims=True) * (1.0 / every)
    root = jnp.sqrt(jnp.float32(every - 1))
    anomalies = (predicted - average) * (scaling / root)
    mismatch = (observed_ref[...] - pred_ref[ens]) * scaling
    spread = sum_ref.shape[2]
    filler = jnp.zeros((spread - every - members, count_obs), jnp.float32)
    sum_ref[0] = dot(anomalies, jnp.concatenate([anomalies, mismatch, filler], axis=0), 1)

    def sum_copy(stage):
        return pltpu.make_async_remote_copy(
            sum_ref.at[stage], sum_land.at[stage], sum_send.at[stage], sum_recv.at[stage],
            device_id={"space": partners[stage]}, device_id_type=MESH,
        )

    for stage in range(stages):
        sum_copy(stage).start()
        sum_copy(stage).wait_recv()
        sum_ref[stage + 1] = sum_ref[stage] + sum_land[stage]

    row_of = lax.broadcasted_iota(jnp.int32, (every, spread), 0)
    lane_of = lax.broadcasted_iota(jnp.int32, (every, spread), 1)
    system = sum_ref[stages] + jnp.where(row_of == lane_of, 1.0, 0.0)
    for pivot in range(every):
        column = system[:, pivot : pivot + 1]
        row = system[pivot : pivot + 1, :]
        row = row / row[:, pivot : pivot + 1]
        system = jnp.where(row_of == pivot, row, system - column * row)
    weights = system[:, every : every + members] / root
    weights = weights - jnp.sum(weights, axis=0, keepdims=True) * (1.0 / every)
    weights = weights.T

    for step in range(enss - 1):
        ens_copy(step).wait()

    @pl.loop(0, rows)
    def _(row):
        block = par_ref[:, row].reshape(every, width)
        own = par_ref[own_groups, row]
        slip_ref[:, row] = own + dot(weights, block, 0).reshape(groups, sub, width)

    for group in range(groups):
        updated_ref[pl.ds(group * sub, sub)] = jnp.swapaxes(slip_ref[group, pl.ds(0, rows)], 0, 1)

    for stage in range(stages):
        sum_copy(stage).wait_send()
    for side in range(2):
        @pl.when(sides[side][0])
        def _(side=side):
            bb_copy(side).wait_send()


def advance(params, bb, counts, cells, observed, noise_var, spaces, enss):
    members, rows, width = params.shape
    groups = members // sub
    total = rows + 2 * halo
    every = members * enss
    count_obs = cells.shape[1]
    spread = pl.cdiv(every + members, lane) * lane
    stages = spaces.bit_length() - 1
    assert 1 << stages == spaces
    dma = pltpu.SemaphoreType.DMA
    vmem = pl.BlockSpec(memory_space=pltpu.VMEM)
    return pl.pallas_call(
        functools.partial(advance_kernel, spaces, enss),
        out_shape=(
            jax.ShapeDtypeStruct(params.shape, jnp.float32),
            jax.ShapeDtypeStruct(params.shape, jnp.float32),
        ),
        in_specs=[vmem] * 6,
        out_specs=(vmem, vmem),
        scratch_shapes=[
            pltpu.VMEM((groups, total, sub, width), jnp.float32),
            pltpu.VMEM((groups, total, sub, width), jnp.float32),
            pltpu.VMEM((total, sub, width), jnp.float32),
            pltpu.VMEM((groups, 2, 2, halo, sub, width), jnp.float32),
            pltpu.VMEM((2, halo, 2, width), jnp.float32),
            pltpu.VMEM((enss * groups, rows, sub, width), jnp.float32),
            pltpu.VMEM((enss, members, count_obs), jnp.float32),
            pltpu.VMEM((stages + 1, every, spread), jnp.float32),
            pltpu.VMEM((stages, every, spread), jnp.float32),
            dma((groups, 2)),
            dma((groups, 2, 2)),
            dma((groups, 2)),
            dma((groups, 2)),
            dma((2,)),
            dma((2,)),
            dma((max(enss - 1, 1),)),
            dma((max(enss - 1, 1),)),
            dma((max(enss - 1, 1),)),
            dma((max(enss - 1, 1),)),
            dma((stages,)),
            dma((stages,)),
        ],
        compiler_params=pltpu.CompilerParams(
            collective_id=0, has_side_effects=True, vmem_limit_bytes=40 * 1024 * 1024
        ),
        name="advance",
    )(params, bb, counts, cells, observed, noise_var)


def shards(params, base_thickness, balance, step_count, obs_index, observed, noise_var):
    members_dev = params.shape[0]
    ens_index = lax.axis_index("ens")
    enss = lax.axis_size("ens")
    own_counts = lax.dynamic_slice_in_dim(step_count, ens_index * members_dev, members_dev)
    counts = jnp.broadcast_to(
        own_counts.reshape(members_dev // sub, sub, 1), (members_dev // sub, sub, lane)
    )
    bb = jnp.stack([base_thickness, balance], axis=1)
    cells = jnp.stack([obs_index // params.shape[2], obs_index % params.shape[2]])
    return advance(
        params, bb, counts, cells, observed[None], noise_var[None], lax.axis_size("space"), enss
    )


def solution(mesh):
    in_specs = (
        P("ens", "space", None),
        P("space", None),
        P("space", None),
        P(),
        P("space"),
        P("space"),
        P("space"),
    )
    out_specs = (P("ens", "space", None), P("ens", "space", None))
    return jax.shard_map(shards, mesh=mesh, in_specs=in_specs, out_specs=out_specs, check_vma=False)
```

```python
import functools
import jax
import jax.numpy as jnp
from jax import lax
from jax.experimental import pallas as pl
from jax.experimental.pallas import tpu as pltpu
from jax.sharding import PartitionSpec as P

time_step = 0.11
steps = 32
halo = 2
sub = 8
lane = 128
MESH = pl.DeviceIdType.MESH


def reciprocal(x):
    r = pl.reciprocal(x, approx=True)
    return r * (2.0 - x * r)


def dot(left, right, right_dim):
    return lax.dot_general(
        left, right, (((1,), (right_dim,)), ((), ())),
        precision=lax.Precision.HIGHEST, preferred_element_type=jnp.float32,
    )


def substep(h_ref, slip_ref, bal_ref, group, first, last, masks, rows):
    pieces = h_ref.shape[-1] // lane
    lanes = lax.broadcasted_iota(jnp.int32, (sub, lane), 1)
    at_end = lanes == lane - 1
    at_start = lanes == 0
    cols = [pl.ds(p * lane, lane) for p in range(pieces)]
    prev = None
    for row in range(first, last):
        h = [h_ref[group, row, :, c] for c in cols]
        d = []
        for p, c in enumerate(cols):
            square = h[p] * h[p]
            d.append(slip_ref[group, row, :, c] * square * reciprocal(1.0 + square))
        if prev is not None:
            prev_h, prev_d, prev_down = prev
            down = [(d[p] + prev_d[p]) * (h[p] - prev_h[p]) for p in range(pieces)]
            if prev_down is not None:
                out = row - 1
                mask = masks[0] if out < halo else masks[1] if out < halo + rows else masks[2]
                h_next = prev_h[1:] + [jnp.where(at_end, 0.0, pltpu.roll(prev_h[0], lane - 1, 1))]
                d_next = prev_d[1:] + [jnp.where(at_end, 0.0, pltpu.roll(prev_d[0], lane - 1, 1))]
                flux = [
                    (d_next[p] + prev_d[p]) * (h_next[p] - prev_h[p]) for p in range(pieces)
                ]
                edge = jnp.where(at_start, prev_d[0] * prev_h[0], pltpu.roll(flux[-1], 1, 1))
                for p, c in enumerate(cols):
                    f_left = edge if p == 0 else flux[p - 1]
                    change = (down[p] - prev_down[p]) + (flux[p] - f_left)
                    moved = (prev_h[p] + bal_ref[out, :, c]) + change
                    h_ref[group, out, :, c] = jnp.where(mask, moved, prev_h[p])
        else:
            down = None
        prev = (h, d, down)


def advance_kernel(
    spaces, enss, params_ref, bb_ref, count_ref, cell_ref, observed_ref, noise_ref, out_ref, updated_ref,
    h_ref, slip_ref, bal_ref, land_ref, bb_land, par_ref, pred_ref, sum_ref, sum_land, order_ref,
    send_sem, recv_sem, slip_send, slip_recv, bb_send, bb_recv, ens_send, ens_recv,
    pred_send, pred_recv, sum_send, sum_recv,
):
    members, rows, width = params_ref.shape
    groups = members // sub
    total = rows + 2 * halo
    blocks = steps // halo
    me = lax.axis_index("space")
    ens = lax.axis_index("ens")
    has_up = me > 0
    has_down = me < spaces - 1
    up = jnp.maximum(me - 1, 0)
    down = jnp.minimum(me + 1, spaces - 1)
    others = [lax.rem(ens + step, enss) for step in range(1, enss)]
    stages = spaces.bit_length() - 1
    partners = []
    for stage in range(stages):
        bit = 1 << stage
        partners.append(me + bit - 2 * bit * lax.rem(lax.div(me, bit), 2))

    pieces = width // lane
    column_of = lax.broadcasted_iota(jnp.int32, (width, lane), 0)
    first_of = lax.broadcasted_iota(jnp.int32, (width, lane), 1) * pieces
    for piece in range(pieces):
        order_ref[:, piece * lane : (piece + 1) * lane] = jnp.where(
            column_of == first_of + piece, 1.0, 0.0
        )

    barrier = pltpu.get_barrier_semaphore()

    @pl.when(has_up)
    def _():
        pl.semaphore_signal(barrier, inc=1, device_id={"space": up}, device_id_type=MESH)

    @pl.when(has_down)
    def _():
        pl.semaphore_signal(barrier, inc=1, device_id={"space": down}, device_id_type=MESH)

    for other in others:
        pl.semaphore_signal(barrier, inc=1, device_id={"ens": other}, device_id_type=MESH)
    for partner in partners:
        pl.semaphore_signal(barrier, inc=1, device_id={"space": partner}, device_id_type=MESH)
    neighbours = has_up.astype(jnp.int32) + has_down.astype(jnp.int32) + (enss - 1) + stages
    pl.semaphore_wait(barrier, neighbours)

    sides = (
        (has_up, up, pl.ds(halo, halo), pl.ds(halo + rows, halo), 1),
        (has_down, down, pl.ds(rows, halo), pl.ds(0, halo), 0),
    )
    own_rows = (pl.ds(0, halo), pl.ds(rows - halo, halo))

    def bb_copy(side):
        _, target, _, _, there = sides[side]
        return pltpu.make_async_remote_copy(
            bb_ref.at[own_rows[side]], bb_land.at[there], bb_send.at[side], bb_recv.at[there],
            device_id={"space": target}, device_id_type=MESH,
        )

    def slip_copy(group, side):
        _, target, source, dest, there = sides[side]
        return pltpu.make_async_remote_copy(
            slip_ref.at[group, source], slip_ref.at[group, dest],
            slip_send.at[group, side], slip_recv.at[group, there],
            device_id={"space": target}, device_id_type=MESH,
        )

    def slip_arrival(group, side):
        _, target, _, _, _ = sides[side]
        here = pl.ds(0, halo) if side == 0 else pl.ds(halo + rows, halo)
        return pltpu.make_async_remote_copy(
            slip_ref.at[group, here], slip_ref.at[group, here],
            slip_send.at[group, side], slip_recv.at[group, side],
            device_id={"space": target}, device_id_type=MESH,
        )

    def h_copy(group, side, slot):
        _, target, source, _, there = sides[side]
        return pltpu.make_async_remote_copy(
            h_ref.at[group, source], land_ref.at[group, slot, there],
            send_sem.at[group, side], recv_sem.at[group, slot, there],
            device_id={"space": target}, device_id_type=MESH,
        )

    def h_arrival(group, side, slot):
        _, target, source, _, _ = sides[side]
        return pltpu.make_async_remote_copy(
            h_ref.at[group, source], land_ref.at[group, slot, side],
            send_sem.at[group, side], recv_sem.at[group, slot, side],
            device_id={"space": target}, device_id_type=MESH,
        )

    def bb_arrival(side):
        _, target, _, _, _ = sides[side]
        return pltpu.make_async_remote_copy(
            bb_ref.at[own_rows[side]], bb_land.at[side], bb_send.at[side], bb_recv.at[side],
            device_id={"space": target}, device_id_type=MESH,
        )

    for side in range(2):
        @pl.when(sides[side][0])
        def _(side=side):
            bb_copy(side).start()

    @pl.loop(0, groups)
    def _(group):
        turned = jnp.swapaxes(params_ref[pl.ds(group * sub, sub)], 0, 1)
        par_ref[ens * groups + group] = turned
        slip = (jnp.exp(turned) * (0.5 * time_step)).reshape(rows * sub, width)
        slip_ref[group, pl.ds(halo, rows)] = dot(slip, order_ref[...], 0).reshape(rows, sub, width)
        for side in range(2):
            @pl.when(sides[side][0])
            def _(side=side):
                slip_copy(group, side).start()

    own_groups = pl.ds(ens * groups, groups)

    def ens_copy(step):
        return pltpu.make_async_remote_copy(
            par_ref.at[own_groups], par_ref.at[own_groups], ens_send.at[step], ens_recv.at[step],
            device_id={"ens": others[step]}, device_id_type=MESH,
        )

    for step in range(enss - 1):
        ens_copy(step).start()

    def wide(row):
        return jnp.broadcast_to(row, (sub, width))

    @pl.loop(0, rows)
    def _(row):
        base = wide(bb_ref[row, 0:1, :])
        for group in range(groups):
            h_ref[group, row + halo] = base
        bal_ref[row + halo] = wide(bb_ref[row, 1:2, :]) * time_step

    for side in range(2):
        begin = 0 if side == 0 else halo + rows

        @pl.when(sides[side][0])
        def _(side=side, begin=begin):
            bb_arrival(side).wait_recv()
            for row in range(halo):
                base = wide(bb_land[side, row, 0:1, :])
                for group in range(groups):
                    h_ref[group, begin + row] = base
                bal_ref[begin + row] = wide(bb_land[side, row, 1:2, :]) * time_step

        @pl.when(jnp.logical_not(sides[side][0]))
        def _(side=side, begin=begin):
            zero = jnp.zeros((sub, width), jnp.float32)
            for row in range(halo):
                for group in range(groups):
                    h_ref[group, begin + row] = zero
                    slip_ref[group, begin + row] = zero
                bal_ref[begin + row] = zero

    @pl.loop(0, blocks)
    def _(block):
        slot = lax.rem(block, 2)

        @pl.loop(0, groups)
        def _(group):
            for side in range(2):
                begin = 0 if side == 0 else halo + rows

                @pl.when(jnp.logical_and(sides[side][0], block == 0))
                def _(side=side):
                    slip_arrival(group, side).wait_recv()

                @pl.when(jnp.logical_and(sides[side][0], block > 0))
                def _(side=side, begin=begin):
                    h_copy(group, side, slot).wait_send()
                    h_arrival(group, side, slot).wait_recv()
                    h_ref[group, pl.ds(begin, halo)] = land_ref[group, slot, side]

            count = count_ref[group]
            counts = (
                count * has_up.astype(jnp.int32), count, count * has_down.astype(jnp.int32)
            )
            @pl.loop(0, halo)
            def _(step):
                now = block * halo + step
                masks = [now < value for value in counts]
                substep(h_ref, slip_ref, bal_ref, group, 0, total, masks, rows)

            for side in range(2):
                @pl.when(jnp.logical_and(sides[side][0], block < blocks - 1))
                def _(side=side):
                    h_copy(group, side, 1 - slot).start()

    for side in range(2):
        @pl.when(sides[side][0])
        def _(side=side):
            for group in range(groups):
                slip_copy(group, side).wait_send()

    cell_row = cell_ref[0:1, :]
    cell_col = cell_ref[1:2, :]
    count_obs = cell_ref.shape[1]
    one_hot = jnp.where(
        lax.broadcasted_iota(jnp.int32, (width, count_obs), 0) == cell_col, 1.0, 0.0
    )
    at_row = lax.broadcasted_iota(jnp.int32, (rows, sub, count_obs), 0) == cell_row
    for group in range(groups):
        cells = h_ref[group, pl.ds(halo, rows)].reshape(rows * sub, width)
        picked = dot(cells, one_hot, 0).reshape(rows, sub, count_obs)
        pred_ref[ens, pl.ds(group * sub, sub)] = jnp.sum(jnp.where(at_row, picked, 0.0), axis=0)

    def pred_copy(step):
        return pltpu.make_async_remote_copy(
            pred_ref.at[ens], pred_ref.at[ens], pred_send.at[step], pred_recv.at[step],
            device_id={"ens": others[step]}, device_id_type=MESH,
        )

    for step in range(enss - 1):
        pred_copy(step).start()
    for group in range(groups):
        cells = h_ref[group, pl.ds(halo, rows)].reshape(rows * sub, width)
        ordered = dot(cells, order_ref[...], 1).reshape(rows, sub, width)
        out_ref[pl.ds(group * sub, sub)] = jnp.swapaxes(ordered, 0, 1)
    for step in range(enss - 1):
        pred_copy(step).wait()

    every = enss * members
    scaling = lax.rsqrt(noise_ref[...])
    predicted = pred_ref[...].reshape(every, count_obs)
    average = jnp.sum(predicted, axis=0, keepdims=True) * (1.0 / every)
    root = jnp.sqrt(jnp.float32(every - 1))
    anomalies = (predicted - average) * (scaling / root)
    mismatch = (observed_ref[...] - pred_ref[ens]) * scaling
    spread = sum_ref.shape[2]
    filler = jnp.zeros((spread - every - members, count_obs), jnp.float32)
    sum_ref[0] = dot(anomalies, jnp.concatenate([anomalies, mismatch, filler], axis=0), 1)

    def sum_copy(stage):
        return pltpu.make_async_remote_copy(
            sum_ref.at[stage], sum_land.at[stage], sum_send.at[stage], sum_recv.at[stage],
            device_id={"space": partners[stage]}, device_id_type=MESH,
        )

    for stage in range(stages):
        sum_copy(stage).start()
        sum_copy(stage).wait_recv()
        sum_ref[stage + 1] = sum_ref[stage] + sum_land[stage]

    row_of = lax.broadcasted_iota(jnp.int32, (every, spread), 0)
    lane_of = lax.broadcasted_iota(jnp.int32, (every, spread), 1)
    system = sum_ref[stages] + jnp.where(row_of == lane_of, 1.0, 0.0)
    for pivot in range(every):
        column = system[:, pivot : pivot + 1]
        row = system[pivot : pivot + 1, :]
        row = row / row[:, pivot : pivot + 1]
        system = jnp.where(row_of == pivot, row, system - column * row)
    weights = system[:, every : every + members] / root
    weights = weights - jnp.sum(weights, axis=0, keepdims=True) * (1.0 / every)
    weights = weights.T

    for step in range(enss - 1):
        ens_copy(step).wait()

    @pl.loop(0, rows)
    def _(row):
        block = par_ref[:, row].reshape(every, width)
        own = par_ref[own_groups, row]
        slip_ref[:, row] = own + dot(weights, block, 0).reshape(groups, sub, width)

    for group in range(groups):
        updated_ref[pl.ds(group * sub, sub)] = jnp.swapaxes(slip_ref[group, pl.ds(0, rows)], 0, 1)

    for stage in range(stages):
        sum_copy(stage).wait_send()
    for side in range(2):
        @pl.when(sides[side][0])
        def _(side=side):
            bb_copy(side).wait_send()


def advance(params, bb, counts, cells, observed, noise_var, spaces, enss):
    members, rows, width = params.shape
    groups = members // sub
    total = rows + 2 * halo
    every = members * enss
    count_obs = cells.shape[1]
    spread = pl.cdiv(every + members, lane) * lane
    stages = spaces.bit_length() - 1
    assert 1 << stages == spaces
    dma = pltpu.SemaphoreType.DMA
    vmem = pl.BlockSpec(memory_space=pltpu.VMEM)
    return pl.pallas_call(
        functools.partial(advance_kernel, spaces, enss),
        out_shape=(
            jax.ShapeDtypeStruct(params.shape, jnp.float32),
            jax.ShapeDtypeStruct(params.shape, jnp.float32),
        ),
        in_specs=[vmem] * 6,
        out_specs=(vmem, vmem),
        scratch_shapes=[
            pltpu.VMEM((groups, total, sub, width), jnp.float32),
            pltpu.VMEM((groups, total, sub, width), jnp.float32),
            pltpu.VMEM((total, sub, width), jnp.float32),
            pltpu.VMEM((groups, 2, 2, halo, sub, width), jnp.float32),
            pltpu.VMEM((2, halo, 2, width), jnp.float32),
            pltpu.VMEM((enss * groups, rows, sub, width), jnp.float32),
            pltpu.VMEM((enss, members, count_obs), jnp.float32),
            pltpu.VMEM((stages + 1, every, spread), jnp.float32),
            pltpu.VMEM((stages, every, spread), jnp.float32),
            pltpu.VMEM((width, width), jnp.float32),
            dma((groups, 2)),
            dma((groups, 2, 2)),
            dma((groups, 2)),
            dma((groups, 2)),
            dma((2,)),
            dma((2,)),
            dma((max(enss - 1, 1),)),
            dma((max(enss - 1, 1),)),
            dma((max(enss - 1, 1),)),
            dma((max(enss - 1, 1),)),
            dma((stages,)),
            dma((stages,)),
        ],
        compiler_params=pltpu.CompilerParams(
            collective_id=0, has_side_effects=True, vmem_limit_bytes=40 * 1024 * 1024
        ),
        name="advance",
    )(params, bb, counts, cells, observed, noise_var)


def shards(params, base_thickness, balance, step_count, obs_index, observed, noise_var):
    members_dev = params.shape[0]
    ens_index = lax.axis_index("ens")
    enss = lax.axis_size("ens")
    own_counts = lax.dynamic_slice_in_dim(step_count, ens_index * members_dev, members_dev)
    counts = jnp.broadcast_to(
        own_counts.reshape(members_dev // sub, sub, 1), (members_dev // sub, sub, lane)
    )
    bb = jnp.stack([base_thickness, balance], axis=1)
    rows, width = base_thickness.shape
    pieces = width // lane
    bb = bb.reshape(rows, 2, lane, pieces).swapaxes(2, 3).reshape(rows, 2, width)
    column = obs_index % width
    cells = jnp.stack([obs_index // width, column % pieces * lane + column // pieces])
    return advance(
        params, bb, counts, cells, observed[None], noise_var[None], lax.axis_size("space"), enss
    )


def solution(mesh):
    in_specs = (
        P("ens", "space", None),
        P("space", None),
        P("space", None),
        P(),
        P("space"),
        P("space"),
        P("space"),
    )
    out_specs = (P("ens", "space", None), P("ens", "space", None))
    return jax.shard_map(shards, mesh=mesh, in_specs=in_specs, out_specs=out_specs, check_vma=False)
```
